128 devices in a mesh: row: 8 (over x, z_lo), col: 16 (over z_hi, y, core).
Axes of the slice: x: 4, y: 4, z: 4 (z_hi: 2, z_lo: 2; z = z_hi * 2 + z_lo), core: 2. Of those that a mesh axis runs over, the one named last changes fastest.
Arguments:
- a_cols: bfloat16 [16384, 8192], P('row', 'col'), may hold values from -6 to 6
- owners: int32 [1024], replicated, may hold values from 0 to 15
- column_slot: int32 [1024], replicated, may hold values from 0 to 511
- update_flag: int32 [1024], replicated, may hold values from 0 to 1
- rescale: float32 [1024], replicated, may hold values from 0.5 to 2
- inverses: bfloat16 [2, 512, 512], replicated, may hold values from -0.0078125 to 0.0078125
- trailing: float32 [16384, 16384], P('row', 'col'), may hold values from -0.15625 to 0.15625
Outputs:
- updated_slab: float32 [16384, 16384], P('row', 'col')
- panels: bfloat16 [16384, 1024], P('row')
The draws below stay inside these ranges and needn't reach their ends.
All inputs are finite; a program needn't handle non-finite values.
Results may differ from the reference program's by a relative error of at most 0.013.
The reference program's roundings to bfloat16 on the way count: a program that leaves them out, or rounds other values in their place, can miss the bound.
Values may be sent and summed in bfloat16 or wider, within the bound.
No kernel may reach another device: no remote copies, remote signals or barrier semaphores. Data moves between devices by JAX's collectives and lax.ppermute only.
A program may use at most 128 MiB of HBM per device.

```python
import math
import jax
import jax.numpy as jnp
import numpy as np
from jax import lax

P_SIZE = 512
K = 1024
NCD = 512
ROWS = 16384
NC = 8192
N_COL = 16


def place_ends(array, own_key, smallest, top_value):
    shape = array.shape
    place = [jax.random.randint(jax.random.fold_in(own_key, axis), (), 0, shape[axis]) for axis in range(len(shape))]
    array = array.at[tuple(place)].set(smallest)
    longest = shape.index(max(shape))
    place[longest] = (place[longest] + 1) % shape[longest]
    return array.at[tuple(place)].set(top_value)


def block_levels(key, extent, cuts, smallest, high):
    factor_of, own = 1.0, jax.random.fold_in(key, 6)
    for dim, blocks in cuts:
        steps = jnp.exp(jax.random.uniform(jax.random.fold_in(own, dim), (blocks,), jnp.float32, smallest / len(cuts), high / len(cuts)))
        factor_of = factor_of * jnp.repeat(steps, extent[dim] // blocks).reshape([-1 if axis == dim else 1 for axis in range(len(extent))])
    return factor_of


def rank_bounds(number_of, slope):
    loads = [(1 << 20) // math.isqrt(standing ** slope) + 1 for standing in range(1, number_of + 1)]
    deviation = 1 + sum(loads) // (1 << 30)
    return np.cumsum(np.array([max(1, weight // deviation) for weight in loads]))


def ranked(key, shape, number_of, slope):
    table = rank_bounds(number_of, slope)
    pick = jax.random.randint(jax.random.fold_in(key, 1), shape, 0, int(table[number_of - 1]))
    standing = jnp.searchsorted(jnp.asarray(table, jnp.int32), pick, side="right")
    return jax.random.permutation(jax.random.fold_in(key, 2), number_of)[standing].astype(jnp.int32)


def centred(stream_key, shape, spread, most, cuts=(), kind=jnp.bfloat16):
    drawn = jax.random.normal(stream_key, shape, jnp.float32) * spread
    if len(cuts) > 0:
        drawn = block_levels(stream_key, shape, cuts, -0.22, 0.18) * drawn
    return jnp.clip(drawn, min=-most, max=most).astype(kind)


def setup_inputs(seed: int = 0) -> dict:
    keys = jax.random.split(jax.random.key(seed), 8)
    a_cols = centred(keys[0], (ROWS, NC), 1.0, 6.0, ((0, 8), (1, 16)))
    owners = place_ends(ranked(keys[1], (K,), N_COL, 2), jax.random.fold_in(keys[1], 3), 0, N_COL - 1).astype(jnp.int32)
    column_slot = place_ends(jax.random.randint(keys[2], (K,), 0, NCD), jax.random.fold_in(keys[2], 1), 0, NCD - 1).astype(jnp.int32)
    update_flag = place_ends(jax.random.randint(keys[3], (K,), 0, 2), jax.random.fold_in(keys[3], 1), 0, 1).astype(jnp.int32)
    rescale = jnp.clip(jnp.exp(jax.random.uniform(keys[4], (K,), jnp.float32, math.log(0.5), math.log(2.0))), 0.5, 2.0)
    inverses = centred(keys[5], (2, P_SIZE, P_SIZE), (0.6 * P_SIZE ** -0.5 * (P_SIZE * ROWS) ** -0.25), 0.0078125)
    trailing = centred(keys[6], (ROWS, ROWS), ((2 * P_SIZE) ** 0.5 * (P_SIZE * ROWS) ** -0.5), 0.15625, ((0, 8), (1, 16)), jnp.float32)
    return dict(a_cols=a_cols, owners=owners, column_slot=column_slot, update_flag=update_flag, rescale=rescale, inverses=inverses, trailing=trailing)


def panel_pass(columns, inverses, signed, reducer):
    width = inverses.shape[1]
    first_cols = columns[:, :width]
    second_cols = columns[:, width:]
    first_panel = jnp.dot(first_cols, inverses[0], preferred_element_type=jnp.float32).astype(jnp.bfloat16)
    gram_block = reducer(lax.dot_general(first_panel, second_cols, (((0,), (0,)), ((), ())), preferred_element_type=jnp.float32))
    weighted = first_panel * signed[:width][None, :]
    coupled = (second_cols.astype(jnp.float32) - jnp.dot(weighted, gram_block.astype(jnp.bfloat16), preferred_element_type=jnp.float32)).astype(jnp.bfloat16)
    second_panel = jnp.dot(coupled, inverses[1], preferred_element_type=jnp.float32).astype(jnp.bfloat16)
    return jnp.concatenate([first_panel, second_panel], axis=1)


def keep_matrix(matrix):
    return matrix


def reference(a_cols, owners, column_slot, update_flag, rescale, inverses, trailing):
    global_index = (owners * NCD + column_slot).astype(jnp.int32)
    picked = jnp.take(a_cols, global_index, axis=1)
    columns = (picked.astype(jnp.float32) * rescale[None, :]).astype(jnp.bfloat16)
    signed = (2 * update_flag - 1).astype(jnp.bfloat16)
    panels = panel_pass(columns, inverses, signed, keep_matrix)
    weighted = panels * signed[None, :]
    update = lax.dot_general(weighted, panels, (((1,), (1,)), ((), ())), preferred_element_type=jnp.float32)
    return trailing + update, panels
```

```python
import jax
import jax.numpy as jnp
from jax import lax
from jax.sharding import PartitionSpec as P


BF = jnp.bfloat16
F32 = jnp.float32


def move(value, route):
    pairs = []
    for x in range(4):
        for zl in range(2):
            for zh in range(2):
                for y in range(4):
                    for k in range(2):
                        x2, zl2, zh2, y2, k2 = route(x, zl, zh, y, k)
                        source = (x * 2 + zl) * 16 + zh * 8 + y * 2 + k
                        target = (x2 % 4 * 2 + zl2) * 16 + zh2 * 8 + y2 % 4 * 2 + k2
                        pairs.append((source, target))
    return lax.ppermute(value, ("row", "col"), pairs)


def other_core(x, zl, zh, y, k):
    return x, zl, zh, y, 1 - k


def other_zh(x, zl, zh, y, k):
    return x, zl, 1 - zh, y, k


def other_zl(x, zl, zh, y, k):
    return x, 1 - zl, zh, y, k


def along_y(step):
    return lambda x, zl, zh, y, k: (x, zl, zh, y + step, k)


def along_x(step):
    return lambda x, zl, zh, y, k: (x + step, zl, zh, y, k)


def flip_x(bit):
    return lambda x, zl, zh, y, k: (x ^ bit, zl, zh, y, k)


def to_strip(x, zl, zh, y, k):
    zh2 = x // 2
    return x + y, zh ^ zl ^ zh2, zh2, (x % 2) * 2 + zl, k


def rows(value, start, count):
    return lax.dynamic_slice_in_dim(value, start, count, 0)


def put(buffer, piece, start):
    return lax.dynamic_update_slice_in_dim(buffer, piece, start, 0)


def mm(a, b):
    return jnp.dot(a, b, preferred_element_type=F32)


def body(a_cols, owners, column_slot, update_flag, rescale, inverses, trailing):
    col = lax.axis_index("col")
    row = lax.axis_index("row")
    k, y, zh = col % 2, (col // 2) % 4, col // 8
    x, zl = row // 2, row % 2
    signed = (2 * update_flag - 1).astype(BF)

    keep = rows(a_cols, k * 1024, 1024)
    got = move(rows(a_cols, (1 - k) * 1024, 1024), other_core)
    both = jnp.concatenate([keep, got], axis=1)
    pieces = [rows(both, y * 256, 256)]
    for step in (1, 2, 3):
        pieces.append(move(rows(both, ((y + step) % 4) * 256, 256), along_y(step)))
    stored = jnp.concatenate(pieces, axis=1)

    ok, oy, oz = owners % 2, (owners // 2) % 4, owners // 8
    place = ((y - oy) % 4) * 1024 + (ok ^ k) * 512 + column_slot
    place = jnp.where(oz == zh, place, -1)
    select = (lax.broadcasted_iota(jnp.int32, (4096, 1024), 0) == place[None, :]).astype(BF)
    mine = (mm(stored, select) * rescale[None, :]).astype(BF)
    cols = mine + move(mine, other_zh)

    fp = mm(cols[:, :512], inverses[0]).astype(BF)
    right = lax.dynamic_slice_in_dim(cols, 512 + zh * 256, 256, 1)
    gram = lax.dot_general(fp, right, (((0,), (0,)), ((), ())), preferred_element_type=F32)
    gram = rows(gram, k * 256, 256) + move(rows(gram, (1 - k) * 256, 256), other_core)
    total = rows(gram, y * 64, 64)
    for step in (1, 2, 3):
        total = total + move(rows(gram, ((y + step) % 4) * 64, 64), along_y(step))
    total = total + move(total, other_zl)
    total = total + move(total, flip_x(1))
    total = total + move(total, flip_x(2))
    low = total.astype(BF)
    low2 = jnp.zeros((64, 512), BF)
    low2 = lax.dynamic_update_slice_in_dim(low2, low, zh * 256, 1)
    low2 = lax.dynamic_update_slice_in_dim(low2, move(low, other_zh), (1 - zh) * 256, 1)
    low3 = put(jnp.zeros((256, 512), BF), low2, y * 64)
    for step in (1, 2, 3):
        low3 = put(low3, move(low2, along_y(step)), ((y - step) % 4) * 64)
    low4 = put(jnp.zeros((512, 512), BF), low3, k * 256)
    gram_low = put(low4, move(low3, other_core), (1 - k) * 256)

    half = put(jnp.zeros((1024, 1024), BF), cols, y * 256)
    for step in (2, 1, 3):
        half = put(half, move(cols, along_y(step)), ((y - step) % 4) * 256)
    block = put(jnp.zeros((2048, 1024), BF), half, k * 1024)
    block = put(block, move(half, other_core), (1 - k) * 1024)

    first = zh * 2 + y // 2
    piece = move(cols, to_strip)
    strip = put(jnp.zeros((1024, 1024), BF), piece, ((x - first) % 4) * 256)
    for step in (2, 1, 3):
        strip = put(strip, move(piece, along_x(step)), ((x - step - first) % 4) * 256)

    def finish(columns):
        first_panel = mm(columns[:, :512], inverses[0]).astype(BF)
        coupled = (
            columns[:, 512:].astype(F32) - mm(first_panel * signed[None, :512], gram_low)
        ).astype(BF)
        second_panel = mm(coupled, inverses[1]).astype(BF)
        return jnp.concatenate([first_panel, second_panel], axis=1)

    panels = finish(block)
    strip_panels = finish(strip)
    update = lax.dot_general(
        panels * signed[None, :],
        strip_panels,
        (((1,), (1,)), ((), ())),
        preferred_element_type=F32,
    )
    return trailing + update, panels


def solution(mesh):
    placed = (P("row", "col"), P(), P(), P(), P(), P(), P("row", "col"))
    return jax.shard_map(
        body,
        mesh=mesh,
        in_specs=placed,
        out_specs=(P("row", "col"), P("row", None)),
        check_vma=False,
    )
```

```python
import jax
import jax.numpy as jnp
from jax import lax
from jax.experimental import pallas as pl
from jax.experimental.pallas import tpu as pltpu
from jax.sharding import PartitionSpec as P


BF = jnp.bfloat16
F32 = jnp.float32


def move(value, route):
    pairs = []
    for x in range(4):
        for zl in range(2):
            for zh in range(2):
                for y in range(4):
                    for k in range(2):
                        x2, zl2, zh2, y2, k2 = route(x, zl, zh, y, k)
                        source = (x * 2 + zl) * 16 + zh * 8 + y * 2 + k
                        target = (x2 % 4 * 2 + zl2) * 16 + zh2 * 8 + y2 % 4 * 2 + k2
                        pairs.append((source, target))
    return lax.ppermute(value, ("row", "col"), pairs)


def other_core(x, zl, zh, y, k):
    return x, zl, zh, y, 1 - k


def other_zh(x, zl, zh, y, k):
    return x, zl, 1 - zh, y, k


def other_zl(x, zl, zh, y, k):
    return x, 1 - zl, zh, y, k


def along_y(step):
    return lambda x, zl, zh, y, k: (x, zl, zh, y + step, k)


def along_x(step):
    return lambda x, zl, zh, y, k: (x + step, zl, zh, y, k)


def flip_x(bit):
    return lambda x, zl, zh, y, k: (x ^ bit, zl, zh, y, k)


def to_strip(x, zl, zh, y, k):
    zh2 = x // 2
    return x + y, zh ^ zl ^ zh2, zh2, (x % 2) * 2 + zl, k


def rows(value, start, count):
    return lax.dynamic_slice_in_dim(value, start, count, 0)


def put(buffer, piece, start):
    return lax.dynamic_update_slice_in_dim(buffer, piece, start, 0)


def mm(a, b):
    return jnp.dot(a, b, preferred_element_type=F32)


def to_chip(step, dz):
    return lambda x, zl, zh, y, k: (x, zl, zh ^ dz, y + step, k)


def finish_kernel(spot, *refs):
    pieces = refs[:12]
    gram_ref, inverse_ref, sign_ref, trailing_ref, out_ref, panel_ref, strip_ref, now_ref = refs[12:]
    t = pl.program_id(0)
    for i in range(12):

        @pl.when(t == i)
        def _():
            now_ref[...] = pieces[i][...]

    sign = sign_ref[...]
    first = mm(now_ref[:, :512], inverse_ref[0]).astype(BF)
    first_signed = first * sign[:, :512]
    coupled = (now_ref[:, 512:].astype(F32) - mm(first_signed, gram_ref[...])).astype(BF)
    second = mm(coupled, inverse_ref[1]).astype(BF)

    @pl.when(t < 4)
    def _():
        at = pl.ds(pl.multiple_of(spot[t] * 256, 256), 256)
        strip_ref[at, :512] = first
        strip_ref[at, 512:] = second

    @pl.when(t >= 4)
    def _():
        panel_ref[:, :512] = first
        panel_ref[:, 512:] = second
        across = (((1,), (1,)), ((), ()))
        update = lax.dot_general(
            first_signed, strip_ref[:, :512], across, preferred_element_type=F32
        )
        update += lax.dot_general(
            second * sign[:, 512:], strip_ref[:, 512:], across, preferred_element_type=F32
        )
        out_ref[...] = trailing_ref[...] + update


def finish(spot, strips, block, gram_low, inverses, sign, trailing):
    def whole(value):
        zeros = (0,) * value.ndim
        return pl.BlockSpec(
            value.shape, lambda t, spot: zeros, pipeline_mode=pl.Buffered(1)
        )

    def tile(width):
        return pl.BlockSpec((256, width), lambda t, spot: (spot[jnp.maximum(t, 4)], 0))

    fixed = [*strips, *block, gram_low, inverses, sign]
    return pl.pallas_call(
        finish_kernel,
        grid_spec=pltpu.PrefetchScalarGridSpec(
            num_scalar_prefetch=1,
            grid=(12,),
            in_specs=[whole(value) for value in fixed] + [tile(1024)],
            out_specs=[tile(1024), tile(1024)],
            scratch_shapes=[pltpu.VMEM((1024, 1024), BF), pltpu.VMEM((256, 1024), BF)],
        ),
        out_shape=(
            jax.ShapeDtypeStruct((2048, 1024), F32),
            jax.ShapeDtypeStruct((2048, 1024), BF),
        ),
        compiler_params=pltpu.CompilerParams(vmem_limit_bytes=40 * 2**20),
        cost_estimate=pl.CostEstimate(
            flops=9_000_000_000, bytes_accessed=26 * 2**20, transcendentals=0
        ),
    )(spot, *fixed, trailing)


def body(a_cols, owners, column_slot, update_flag, rescale, inverses, trailing):
    col = lax.axis_index("col")
    row = lax.axis_index("row")
    k, y, zh = col % 2, (col // 2) % 4, col // 8
    x, zl = row // 2, row % 2
    signed = (2 * update_flag - 1).astype(BF)

    keep = rows(a_cols, k * 1024, 1024)
    got = move(rows(a_cols, (1 - k) * 1024, 1024), other_core)
    both = jnp.concatenate([keep, got], axis=1)
    ok, oy, oz = owners % 2, (owners // 2) % 4, owners // 8
    place = (ok ^ k) * 512 + column_slot
    slots = lax.broadcasted_iota(jnp.int32, (1024, 1024), 0)
    picked = None
    for dz in (0, 1):
        for step in (0, 1, 2, 3):
            piece = rows(both, (y + step) % 4 * 256 + (zh ^ dz) * 128, 128)
            if dz or step:
                piece = move(piece, to_chip(step, dz))
            held = (oz == (zh ^ dz)) & ((y - oy) % 4 == step)
            select = (slots == jnp.where(held, place, -1)[None, :]).astype(BF)
            term = mm(piece, select)
            picked = term if picked is None else picked + term
    cols = (picked * rescale[None, :]).astype(BF)

    pair = put(jnp.zeros((256, 1024), BF), cols, zh * 128)
    pair = put(pair, move(cols, other_zh), (1 - zh) * 128)

    first = zh * 2 + y // 2
    part = zl ^ (y % 2) ^ zh
    piece = move(cols, to_strip)
    strip = put(jnp.zeros((256, 1024), BF), piece, part * 128)
    strip = put(strip, move(piece, other_zl), (1 - part) * 128)
    strips = [strip] + [move(strip, along_x(step)) for step in (1, 2, 3)]

    near = [pair] + [move(pair, along_y(step)) for step in (1, 2, 3)]
    far = [move(value, other_core) for value in near]

    fp = mm(pair[:, :512], inverses[0]).astype(BF)
    right = lax.dynamic_slice_in_dim(pair, 512 + zh * 256, 256, 1)
    gram = lax.dot_general(fp, right, (((0,), (0,)), ((), ())), preferred_element_type=F32)
    gram = rows(gram, k * 256, 256) + move(rows(gram, (1 - k) * 256, 256), other_core)
    total = rows(gram, y * 64, 64)
    for step in (1, 2, 3):
        total = total + move(rows(gram, ((y + step) % 4) * 64, 64), along_y(step))
    total = total + move(total, other_zl)
    total = total + move(total, flip_x(1))
    total = total + move(total, flip_x(2))
    low = total.astype(BF)
    low2 = jnp.zeros((64, 512), BF)
    low2 = lax.dynamic_update_slice_in_dim(low2, low, zh * 256, 1)
    low2 = lax.dynamic_update_slice_in_dim(low2, move(low, other_zh), (1 - zh) * 256, 1)
    low3 = put(jnp.zeros((256, 512), BF), low2, y * 64)
    for step in (1, 2, 3):
        low3 = put(low3, move(low2, along_y(step)), ((y - step) % 4) * 64)
    low4 = put(jnp.zeros((512, 512), BF), low3, k * 256)
    gram_low = put(low4, move(low3, other_core), (1 - k) * 256)

    tile = lax.iota(jnp.int32, 12)
    step = tile % 4
    spot = jnp.where(
        tile < 4,
        (x - step - first) % 4,
        jnp.where(tile < 8, k, 1 - k) * 4 + (y - step) % 4,
    )
    return finish(spot, strips, near + far, gram_low, inverses, signed[None, :], trailing)


def solution(mesh):
    placed = (P("row", "col"), P(), P(), P(), P(), P(), P("row", "col"))
    return jax.shard_map(
        body,
        mesh=mesh,
        in_specs=placed,
        out_specs=(P("row", "col"), P("row", None)),
        check_vma=False,
    )
```

```python
import jax
import jax.numpy as jnp
from jax import lax
from jax.experimental import pallas as pl
from jax.experimental.pallas import tpu as pltpu
from jax.sharding import PartitionSpec as P


BF = jnp.bfloat16
F32 = jnp.float32


def move(value, route):
    pairs = []
    for x in range(4):
        for zl in range(2):
            for zh in range(2):
                for y in range(4):
                    for k in range(2):
                        x2, zl2, zh2, y2, k2 = route(x, zl, zh, y, k)
                        source = (x * 2 + zl) * 16 + zh * 8 + y * 2 + k
                        target = (x2 % 4 * 2 + zl2) * 16 + zh2 * 8 + y2 % 4 * 2 + k2
                        pairs.append((source, target))
    return lax.ppermute(value, ("row", "col"), pairs)


def other_core(x, zl, zh, y, k):
    return x, zl, zh, y, 1 - k


def other_zh(x, zl, zh, y, k):
    return x, zl, 1 - zh, y, k


def other_zl(x, zl, zh, y, k):
    return x, 1 - zl, zh, y, k


def along_y(step):
    return lambda x, zl, zh, y, k: (x, zl, zh, y + step, k)


def along_x(step):
    return lambda x, zl, zh, y, k: (x + step, zl, zh, y, k)


def flip_x(bit):
    return lambda x, zl, zh, y, k: (x ^ bit, zl, zh, y, k)


def to_strip(x, zl, zh, y, k):
    zh2 = x // 2
    return x + y, zh ^ zl ^ zh2, zh2, (x % 2) * 2 + zl, k


def rows(value, start, count):
    return lax.dynamic_slice_in_dim(value, start, count, 0)


def put(buffer, piece, start):
    return lax.dynamic_update_slice_in_dim(buffer, piece, start, 0)


def mm(a, b):
    return jnp.dot(a, b, preferred_element_type=F32)


def to_chip(step, dz):
    return lambda x, zl, zh, y, k: (x, zl, zh ^ dz, y + step, k)


def panel(cols, inverses, gram, sign):
    first = mm(cols[:, :512], inverses[0]).astype(BF)
    weighted = first * sign[:, :512]
    coupled = (cols[:, 512:].astype(F32) - mm(weighted, gram[...])).astype(BF)
    return first, mm(coupled, inverses[1]).astype(BF)


def whole(value):
    zeros = (0,) * value.ndim
    return pl.BlockSpec(value.shape, lambda t, spot: zeros, pipeline_mode=pl.Buffered(1))


def block_kernel(spot, *refs):
    pieces = refs[:8]
    gram, inverses, sign, out, now = refs[8:]
    for half in range(2):

        @pl.when(pl.program_id(0) == half)
        def _():
            for i in range(4):
                at = pl.ds(pl.multiple_of(spot[half * 4 + i] % 4 * 256, 256), 256)
                now[at, :] = pieces[half * 4 + i][...]

    for at in (slice(0, 512), slice(512, 1024)):
        first, second = panel(now.at[at], inverses, gram, sign[...])
        out[at, :512] = first
        out[at, 512:] = second


def block_panels(spot, pieces, gram, inverses, sign):
    fixed = [*pieces, gram, inverses, sign]
    return pl.pallas_call(
        block_kernel,
        grid_spec=pltpu.PrefetchScalarGridSpec(
            num_scalar_prefetch=1,
            grid=(2,),
            in_specs=[whole(value) for value in fixed],
            out_specs=pl.BlockSpec((1024, 1024), lambda t, spot: (spot[4 * t] // 4, 0)),
            scratch_shapes=[pltpu.VMEM((1024, 1024), BF)],
        ),
        out_shape=jax.ShapeDtypeStruct((2048, 1024), BF),
        compiler_params=pltpu.CompilerParams(vmem_limit_bytes=32 * 2**20),
        cost_estimate=pl.CostEstimate(
            flops=3_200_000_000, bytes_accessed=9 * 2**20, transcendentals=0
        ),
    )(spot, *fixed)


SLAB = 512
SLABS = 2048 // SLAB


def slab_kernel(spot, *refs):
    strips = refs[:5]
    gram, inverses, sign, panels, trailing, out = refs[5:11]
    cols, strip, panel_here, slab, panel_sem, load_sem, save_sem = refs[11:]

    def loads(i):
        at = pl.ds(i * SLAB, SLAB)
        return (
            pltpu.make_async_copy(panels.at[at], panel_here.at[at], panel_sem.at[i]),
            pltpu.make_async_copy(trailing.at[at], slab.at[at], load_sem.at[i]),
        )

    def save(i):
        at = pl.ds(i * SLAB, SLAB)
        return pltpu.make_async_copy(slab.at[at], out.at[at], save_sem.at[i])

    for i in range(SLABS):
        for copy in loads(i):
            copy.start()
    for i, piece in enumerate(strips):
        height = piece.shape[0]
        cols[pl.ds(pl.multiple_of(spot[i] * 128, 128), height), :] = piece[...]
    first, second = panel(cols, inverses, gram, sign[...])
    strip[:, :512] = first * sign[:, :512]
    strip[:, 512:] = second * sign[:, 512:]

    def step(i, carry):
        for copy in loads(i):
            copy.wait()
        at = pl.ds(pl.multiple_of(i * SLAB, SLAB), SLAB)
        slab[at, :] = slab[at, :] + lax.dot_general(
            panel_here[at, :],
            strip[...],
            (((1,), (1,)), ((), ())),
            preferred_element_type=F32,
        )
        save(i).start()
        return carry

    lax.fori_loop(0, SLABS, step, 0)
    for i in range(SLABS):
        save(i).wait()


def update_slab(spot, strips, gram, inverses, sign, panels, trailing):
    fixed = [*strips, gram, inverses, sign]
    anywhere = pl.BlockSpec(memory_space=pl.ANY)
    return pl.pallas_call(
        slab_kernel,
        grid_spec=pltpu.PrefetchScalarGridSpec(
            num_scalar_prefetch=1,
            grid=(1,),
            in_specs=[whole(value) for value in fixed] + [anywhere] * 2,
            out_specs=anywhere,
            scratch_shapes=[
                pltpu.VMEM((1024, 1024), BF),
                pltpu.VMEM((1024, 1024), BF),
                pltpu.VMEM((2048, 1024), BF),
                pltpu.VMEM((2048, 1024), F32),
                pltpu.SemaphoreType.DMA((SLABS,)),
                pltpu.SemaphoreType.DMA((SLABS,)),
                pltpu.SemaphoreType.DMA((SLABS,)),
            ],
        ),
        out_shape=jax.ShapeDtypeStruct((2048, 1024), F32),
        compiler_params=pltpu.CompilerParams(vmem_limit_bytes=58 * 2**20),
        cost_estimate=pl.CostEstimate(
            flops=6_000_000_000, bytes_accessed=24 * 2**20, transcendentals=0
        ),
    )(spot, *fixed, panels, trailing)


def body(a_cols, owners, column_slot, update_flag, rescale, inverses, trailing):
    col = lax.axis_index("col")
    row = lax.axis_index("row")
    k, y, zh = col % 2, (col // 2) % 4, col // 8
    x, zl = row // 2, row % 2
    signed = (2 * update_flag - 1).astype(BF)

    keep = rows(a_cols, k * 1024, 1024)
    got = move(rows(a_cols, (1 - k) * 1024, 1024), other_core)
    both = jnp.concatenate([keep, got], axis=1)
    ok, oy, oz = owners % 2, (owners // 2) % 4, owners // 8
    place = (ok ^ k) * 512 + column_slot
    slots = lax.broadcasted_iota(jnp.int32, (1024, 1024), 0)
    picked = None
    for dz in (0, 1):
        for step in (0, 1, 2, 3):
            piece = rows(both, (y + step) % 4 * 256 + (zh ^ dz) * 128, 128)
            if dz or step:
                piece = move(piece, to_chip(step, dz))
            held = (oz == (zh ^ dz)) & ((y - oy) % 4 == step)
            select = (slots == jnp.where(held, place, -1)[None, :]).astype(BF)
            term = mm(piece, select)
            picked = term if picked is None else picked + term
    cols = (picked * rescale[None, :]).astype(BF)

    pair = put(jnp.zeros((256, 1024), BF), cols, zh * 128)
    pair = put(pair, move(cols, other_zh), (1 - zh) * 128)

    first = zh * 2 + y // 2
    part = zl ^ (y % 2) ^ zh
    piece = move(cols, to_strip)
    strip = put(jnp.zeros((256, 1024), BF), piece, part * 128)
    strip = put(strip, move(piece, other_zl), (1 - part) * 128)
    strips = [strip] + [move(strip, along_x(step)) for step in (1, 3)]
    across = move(piece, along_x(2))
    strips += [across, move(across, other_zl)]

    near = [pair] + [move(pair, along_y(step)) for step in (1, 2, 3)]
    far = [move(value, other_core) for value in near]

    fp = mm(pair[:, :512], inverses[0]).astype(BF)
    right = lax.dynamic_slice_in_dim(pair, 512 + zh * 256, 256, 1)
    gram = lax.dot_general(fp, right, (((0,), (0,)), ((), ())), preferred_element_type=F32)
    gram = rows(gram, k * 256, 256) + move(rows(gram, (1 - k) * 256, 256), other_core)
    total = rows(gram, y * 64, 64)
    for step in (1, 2, 3):
        total = total + move(rows(gram, ((y + step) % 4) * 64, 64), along_y(step))
    total = total + move(total, other_zl)
    total = total + move(total, flip_x(1))
    total = total + move(total, flip_x(2))
    low = total.astype(BF)
    low2 = jnp.zeros((64, 512), BF)
    low2 = lax.dynamic_update_slice_in_dim(low2, low, zh * 256, 1)
    low2 = lax.dynamic_update_slice_in_dim(low2, move(low, other_zh), (1 - zh) * 256, 1)
    low3 = put(jnp.zeros((256, 512), BF), low2, y * 64)
    for step in (1, 2, 3):
        low3 = put(low3, move(low2, along_y(step)), ((y - step) % 4) * 64)
    low4 = put(jnp.zeros((512, 512), BF), low3, k * 256)
    gram_low = put(low4, move(low3, other_core), (1 - k) * 256)

    index = lax.iota(jnp.int32, 8)
    block_spot = jnp.where(index < 4, k, 1 - k) * 4 + (y - index) % 4
    hop = jnp.where(index < 3, (index * index + index) // 2, 2)
    lower = jnp.where(index == 3, part, jnp.where(index == 4, 1 - part, 0))
    strip_spot = (x - hop - first) % 4 * 2 + lower
    sign = signed[None, :]
    panels = block_panels(block_spot, near + far, gram_low, inverses, sign)
    slab = update_slab(strip_spot, strips, gram_low, inverses, sign, panels, trailing)
    return slab, panels


def solution(mesh):
    placed = (P("row", "col"), P(), P(), P(), P(), P(), P("row", "col"))
    return jax.shard_map(
        body,
        mesh=mesh,
        in_specs=placed,
        out_specs=(P("row", "col"), P("row", None)),
        check_vma=False,
    )
```

```python
import jax
import jax.numpy as jnp
from jax import lax
from jax.experimental import pallas as pl
from jax.experimental.pallas import tpu as pltpu
from jax.sharding import PartitionSpec as P


BF = jnp.bfloat16
F32 = jnp.float32


def move(value, route):
    pairs = []
    for x in range(4):
        for zl in range(2):
            for zh in range(2):
                for y in range(4):
                    for k in range(2):
                        x2, zl2, zh2, y2, k2 = route(x, zl, zh, y, k)
                        source = (x * 2 + zl) * 16 + zh * 8 + y * 2 + k
                        target = (x2 % 4 * 2 + zl2) * 16 + zh2 * 8 + y2 % 4 * 2 + k2
                        pairs.append((source, target))
    return lax.ppermute(value, ("row", "col"), pairs)


def other_core(x, zl, zh, y, k):
    return x, zl, zh, y, 1 - k


def other_zh(x, zl, zh, y, k):
    return x, zl, 1 - zh, y, k


def other_zl(x, zl, zh, y, k):
    return x, 1 - zl, zh, y, k


def along_y(step):
    return lambda x, zl, zh, y, k: (x, zl, zh, y + step, k)


def along_x(step):
    return lambda x, zl, zh, y, k: (x + step, zl, zh, y, k)


def flip_x(bit):
    return lambda x, zl, zh, y, k: (x ^ bit, zl, zh, y, k)


def to_strip(x, zl, zh, y, k):
    zh2 = x // 2
    return x + y, zh ^ zl ^ zh2, zh2, (x % 2) * 2 + zl, k


def rows(value, start, count):
    return lax.dynamic_slice_in_dim(value, start, count, 0)


def put(buffer, piece, start):
    return lax.dynamic_update_slice_in_dim(buffer, piece, start, 0)


def mm(a, b):
    return jnp.dot(a, b, preferred_element_type=F32)


def to_chip(step, dz):
    return lambda x, zl, zh, y, k: (x, zl, zh ^ dz, y + step, k)


def panel(cols, inverses, gram, sign):
    first = mm(cols[:, :512], inverses[0]).astype(BF)
    weighted = first * sign[:, :512]
    coupled = (cols[:, 512:].astype(F32) - mm(weighted, gram[...])).astype(BF)
    return first, mm(coupled, inverses[1]).astype(BF)


SLAB = 512
SLABS = 2048 // SLAB


def tail_kernel(spot, *refs):
    pieces = refs[:17]
    inverses, sign, trailing, out, panels = refs[17:22]
    cols, strip, block, panel_here, slab, gram_here, inverses_here = refs[22:29]
    piece_sem, fixed_sem, load_sem, save_sem, panel_sem = refs[29:]

    def fetch(i):
        height = pieces[i].shape[0]
        at = pl.ds(pl.multiple_of(spot[i] * 128, 128), height)
        target = cols if i < 5 else block if i < 15 else gram_here
        return pltpu.make_async_copy(pieces[i], target.at[at], piece_sem.at[i])

    def rows_of(i):
        return pl.ds(pl.multiple_of(i * SLAB, SLAB), SLAB)

    def load(i):
        return pltpu.make_async_copy(
            trailing.at[rows_of(i)], slab.at[rows_of(i)], load_sem.at[i]
        )

    def save(i):
        return pltpu.make_async_copy(slab.at[rows_of(i)], out.at[rows_of(i)], save_sem.at[i])

    def save_panel(i):
        return pltpu.make_async_copy(
            panel_here.at[rows_of(i)], panels.at[rows_of(i)], panel_sem.at[i]
        )

    constants = pltpu.make_async_copy(inverses, inverses_here, fixed_sem)
    constants.start()
    early = (0, 1, 2, 3, 4, 15, 16)
    for i in early:
        fetch(i).start()
    for i in range(5, 15):
        fetch(i).start()
    for i in range(SLABS):
        load(i).start()

    for i in early:
        fetch(i).wait()
    constants.wait()
    first, second = panel(cols, inverses_here, gram_here, sign[...])
    strip[:, :512] = first * sign[:, :512]
    strip[:, 512:] = second * sign[:, 512:]
    for i in range(5, 15):
        fetch(i).wait()

    def step(i, carry):
        at = rows_of(i)
        first, second = panel(block.at[at], inverses_here, gram_here, sign[...])
        panel_here[at, :512] = first
        panel_here[at, 512:] = second
        save_panel(i).start()
        load(i).wait()
        slab[at, :] = slab[at, :] + lax.dot_general(
            panel_here[at, :],
            strip[...],
            (((1,), (1,)), ((), ())),
            preferred_element_type=F32,
        )
        save(i).start()
        return carry

    lax.fori_loop(0, SLABS, step, 0)
    for i in range(SLABS):
        save_panel(i).wait()
        save(i).wait()


def tail(spot, pieces, inverses, sign, trailing):
    anywhere = pl.BlockSpec(memory_space=pl.ANY)
    return pl.pallas_call(
        tail_kernel,
        grid_spec=pltpu.PrefetchScalarGridSpec(
            num_scalar_prefetch=1,
            grid=(1,),
            in_specs=[anywhere] * 18
            + [pl.BlockSpec((1, 1024), lambda t, spot: (0, 0)), anywhere],
            out_specs=[anywhere] * 2,
            scratch_shapes=[
                pltpu.VMEM((1024, 1024), BF),
                pltpu.VMEM((1024, 1024), BF),
                pltpu.VMEM((2048, 1024), BF),
                pltpu.VMEM((2048, 1024), BF),
                pltpu.VMEM((2048, 1024), F32),
                pltpu.VMEM((512, 512), BF),
                pltpu.VMEM((2, 512, 512), BF),
                pltpu.SemaphoreType.DMA((17,)),
                pltpu.SemaphoreType.DMA,
                pltpu.SemaphoreType.DMA((SLABS,)),
                pltpu.SemaphoreType.DMA((SLABS,)),
                pltpu.SemaphoreType.DMA((SLABS,)),
            ],
        ),
        out_shape=(
            jax.ShapeDtypeStruct((2048, 1024), F32),
            jax.ShapeDtypeStruct((2048, 1024), BF),
        ),
        compiler_params=pltpu.CompilerParams(vmem_limit_bytes=46 * 2**20),
        cost_estimate=pl.CostEstimate(
            flops=9_000_000_000, bytes_accessed=28 * 2**20, transcendentals=0
        ),
    )(spot, *pieces, inverses, sign, trailing)


def body(a_cols, owners, column_slot, update_flag, rescale, inverses, trailing):
    col = lax.axis_index("col")
    row = lax.axis_index("row")
    k, y, zh = col % 2, (col // 2) % 4, col // 8
    x, zl = row // 2, row % 2
    signed = (2 * update_flag - 1).astype(BF)

    keep = rows(a_cols, k * 1024, 1024)
    got = move(rows(a_cols, (1 - k) * 1024, 1024), other_core)
    both = jnp.concatenate([keep, got], axis=1)
    ok, oy, oz = owners % 2, (owners // 2) % 4, owners // 8
    place = (ok ^ k) * 512 + column_slot
    slots = lax.broadcasted_iota(jnp.int32, (1024, 1024), 0)
    picked = None
    for dz in (0, 1):
        for step in (0, 1, 2, 3):
            piece = rows(both, (y + step) % 4 * 256 + (zh ^ dz) * 128, 128)
            if dz or step:
                piece = move(piece, to_chip(step, dz))
            held = (oz == (zh ^ dz)) & ((y - oy) % 4 == step)
            select = (slots == jnp.where(held, place, -1)[None, :]).astype(BF)
            term = mm(piece, select)
            picked = term if picked is None else picked + term
    cols = (picked * rescale[None, :]).astype(BF)

    pair = put(jnp.zeros((256, 1024), BF), cols, zh * 128)
    pair = put(pair, move(cols, other_zh), (1 - zh) * 128)

    first = zh * 2 + y // 2
    part = zl ^ (y % 2) ^ zh
    piece = move(cols, to_strip)
    strip = put(jnp.zeros((256, 1024), BF), piece, part * 128)
    strip = put(strip, move(piece, other_zl), (1 - part) * 128)
    strips = [strip] + [move(strip, along_x(step)) for step in (1, 3)]
    across = move(piece, along_x(2))
    strips += [across, move(across, other_zl)]

    beyond = move(cols, along_y(2))
    near = [pair] + [move(pair, along_y(step)) for step in (1, 3)]
    near += [beyond, move(beyond, other_zh)]
    far = [move(value, other_core) for value in near]

    fp = mm(pair[:, :512], inverses[0]).astype(BF)
    right = lax.dynamic_slice_in_dim(pair, 512 + zh * 256, 256, 1)
    gram = lax.dot_general(fp, right, (((0,), (0,)), ((), ())), preferred_element_type=F32)
    gram = rows(gram, k * 256, 256) + move(rows(gram, (1 - k) * 256, 256), other_core)
    total = rows(gram, y * 64, 64)
    for step in (1, 2, 3):
        total = total + move(rows(gram, ((y + step) % 4) * 64, 64), along_y(step))
    total = total + move(total, other_zl)
    one, two, three = [move(total, flip_x(bit)) for bit in (1, 2, 3)]
    total = (total + one) + (two + three)
    low = total.astype(BF)
    low2 = jnp.zeros((64, 512), BF)
    low2 = lax.dynamic_update_slice_in_dim(low2, low, zh * 256, 1)
    low2 = lax.dynamic_update_slice_in_dim(low2, move(low, other_zh), (1 - zh) * 256, 1)
    low3 = put(jnp.zeros((256, 512), BF), low2, y * 64)
    for step in (1, 2, 3):
        low3 = put(low3, move(low2, along_y(step)), ((y - step) % 4) * 64)
    grams = [low3, move(low3, other_core)]

    index = lax.iota(jnp.int32, 15)
    kind, index = index // 5, index % 5
    hop = jnp.where(index < 3, (index * index + index) // 2, 2)
    half = jnp.where(kind == 0, part, zh)
    lower = jnp.where(index == 3, half, jnp.where(index == 4, 1 - half, 0))
    base = jnp.where(kind == 0, x - first, y)
    spot = (base - hop) % 4 * 2 + lower
    spot += jnp.where(kind == 0, 0, jnp.where(kind == 1, k, 1 - k)) * 8
    spot = jnp.concatenate([spot, jnp.stack([k, 1 - k]) * 2])
    return tail(spot, strips + near + far + grams, inverses, signed[None, :], trailing)


def solution(mesh):
    placed = (P("row", "col"), P(), P(), P(), P(), P(), P("row", "col"))
    return jax.shard_map(
        body,
        mesh=mesh,
        in_specs=placed,
        out_specs=(P("row", "col"), P("row", None)),
        check_vma=False,
    )
```

```python
import jax
import jax.numpy as jnp
from jax import lax
from jax.experimental import pallas as pl
from jax.experimental.pallas import tpu as pltpu
from jax.sharding import PartitionSpec as P


BF = jnp.bfloat16
F32 = jnp.float32


def move(value, route):
    pairs = []
    for x in range(4):
        for zl in range(2):
            for zh in range(2):
                for y in range(4):
                    for k in range(2):
                        x2, zl2, zh2, y2, k2 = route(x, zl, zh, y, k)
                        source = (x * 2 + zl) * 16 + zh * 8 + y * 2 + k
                        target = (x2 % 4 * 2 + zl2) * 16 + zh2 * 8 + y2 % 4 * 2 + k2
                        pairs.append((source, target))
    return lax.ppermute(value, ("row", "col"), pairs)


def other_core(x, zl, zh, y, k):
    return x, zl, zh, y, 1 - k


def other_zh(x, zl, zh, y, k):
    return x, zl, 1 - zh, y, k


def other_zl(x, zl, zh, y, k):
    return x, 1 - zl, zh, y, k


def along_y(step):
    return lambda x, zl, zh, y, k: (x, zl, zh, y + step, k)


def along_x(step):
    return lambda x, zl, zh, y, k: (x + step, zl, zh, y, k)


def flip_x(bit):
    return lambda x, zl, zh, y, k: (x ^ bit, zl, zh, y, k)


def flip_y(bit):
    return lambda x, zl, zh, y, k: (x, zl, zh, y ^ bit, k)


def to_strip(x, zl, zh, y, k):
    zh2 = x // 2
    return x + y, zh ^ zl ^ zh2, zh2, (x % 2) * 2 + zl, k


def rows(value, start, count):
    return lax.dynamic_slice_in_dim(value, start, count, 0)


def joined(mine, theirs, mine_second, axis):
    return jnp.where(
        mine_second == 1,
        jnp.concatenate([theirs, mine], axis),
        jnp.concatenate([mine, theirs], axis),
    )


def mm(a, b):
    return jnp.dot(a, b, preferred_element_type=F32)


def to_chip(step, dz):
    return lambda x, zl, zh, y, k: (x, zl, zh ^ dz, y + step, k)


def second_panel(cols, inverse, gram, sign):
    weighted = cols[:, :512] * sign[:, :512]
    coupled = (cols[:, 512:].astype(F32) - mm(weighted, gram[...])).astype(BF)
    return mm(coupled, inverse[...]).astype(BF)


SLAB = 512
SLABS = 2048 // SLAB


def tail_kernel(spot, *refs):
    pieces = refs[:17]
    inverses, sign, trailing, out, panels = refs[17:22]
    cols, strip, block, slab, gram_here, inverse_here = refs[22:28]
    piece_sem, fixed_sem, load_sem, save_sem, panel_sem = refs[28:]

    def fetch(i):
        if i >= 24:
            source, target, height = pieces[15 + i - 24], gram_here, 256
        else:
            group, half = i // 8, i % 8
            source = pieces[group * 5 + (half // 2 if half < 6 else half - 3)]
            if half < 6:
                source = source.at[pl.ds(half % 2 * 128, 128)]
            target, height = cols if group == 0 else block, 128
        at = pl.ds(pl.multiple_of(spot[i] * 128, 128), height)
        return pltpu.make_async_copy(source, target.at[at], piece_sem.at[i])

    def rows_of(i):
        return pl.ds(pl.multiple_of(i * SLAB, SLAB), SLAB)

    def load(i):
        return pltpu.make_async_copy(
            trailing.at[rows_of(i)], slab.at[rows_of(i)], load_sem.at[i]
        )

    def save(i):
        return pltpu.make_async_copy(slab.at[rows_of(i)], out.at[rows_of(i)], save_sem.at[i])

    def save_panel(i):
        return pltpu.make_async_copy(
            block.at[rows_of(i)], panels.at[rows_of(i)], panel_sem.at[i]
        )

    constants = pltpu.make_async_copy(inverses.at[1], inverse_here, fixed_sem)
    constants.start()
    early = (*range(8), 24, 25)
    for i in early:
        fetch(i).start()
    for i in range(8, 24):
        fetch(i).start()
    for i in range(SLABS):
        load(i).start()

    for i in early:
        fetch(i).wait()
    constants.wait()
    second = second_panel(cols, inverse_here, gram_here, sign[...])
    strip[:, :512] = cols[:, :512] * sign[:, :512]
    strip[:, 512:] = second * sign[:, 512:]
    for i in range(8, 24):
        fetch(i).wait()

    def step(i, carry):
        at = rows_of(i)
        block[at, 512:] = second_panel(block.at[at], inverse_here, gram_here, sign[...])
        save_panel(i).start()
        load(i).wait()
        slab[at, :] = slab[at, :] + lax.dot_general(
            block[at, :],
            strip[...],
            (((1,), (1,)), ((), ())),
            preferred_element_type=F32,
        )
        save(i).start()
        return carry

    lax.fori_loop(0, SLABS, step, 0)
    for i in range(SLABS):
        save_panel(i).wait()
        save(i).wait()


def tail(spot, pieces, inverses, sign, trailing):
    anywhere = pl.BlockSpec(memory_space=pl.ANY)
    return pl.pallas_call(
        tail_kernel,
        grid_spec=pltpu.PrefetchScalarGridSpec(
            num_scalar_prefetch=1,
            grid=(1,),
            in_specs=[anywhere] * 18
            + [pl.BlockSpec((1, 1024), lambda t, spot: (0, 0)), anywhere],
            out_specs=[anywhere] * 2,
            scratch_shapes=[
                pltpu.VMEM((1024, 1024), BF),
                pltpu.VMEM((1024, 1024), BF),
                pltpu.VMEM((2048, 1024), BF),
                pltpu.VMEM((2048, 1024), F32),
                pltpu.VMEM((512, 512), BF),
                pltpu.VMEM((512, 512), BF),
                pltpu.SemaphoreType.DMA((26,)),
                pltpu.SemaphoreType.DMA,
                pltpu.SemaphoreType.DMA((SLABS,)),
                pltpu.SemaphoreType.DMA((SLABS,)),
                pltpu.SemaphoreType.DMA((SLABS,)),
            ],
        ),
        out_shape=(
            jax.ShapeDtypeStruct((2048, 1024), F32),
            jax.ShapeDtypeStruct((2048, 1024), BF),
        ),
        compiler_params=pltpu.CompilerParams(vmem_limit_bytes=46 * 2**20),
        cost_estimate=pl.CostEstimate(
            flops=9_000_000_000, bytes_accessed=28 * 2**20, transcendentals=0
        ),
    )(spot, *pieces, inverses, sign, trailing)


def body(a_cols, owners, column_slot, update_flag, rescale, inverses, trailing):
    col = lax.axis_index("col")
    row = lax.axis_index("row")
    k, y, zh = col % 2, (col // 2) % 4, col // 8
    x, zl = row // 2, row % 2
    signed = (2 * update_flag - 1).astype(BF)

    keep = rows(a_cols, k * 1024, 1024)
    got = move(rows(a_cols, (1 - k) * 1024, 1024), other_core)
    chip = owners // 2
    stored = (owners % 2 ^ k) * 512 + column_slot
    square = (1024, 1024)
    before = lax.broadcasted_iota(jnp.int32, square, 0) < lax.broadcasted_iota(jnp.int32, square, 1)
    rank = jnp.sum((chip[:, None] == chip[None, :]) & before, axis=0, dtype=jnp.int32)

    def exchange(base):
        slot = lax.broadcasted_iota(jnp.int32, (1024, 512), 1)
        held = (chip == zh * 4 + y)[:, None] & ((rank - base)[:, None] == slot)
        origin = jnp.sum(jnp.where(held, stored[:, None] + 1, 0), axis=0) - 1
        pack = (lax.broadcasted_iota(jnp.int32, (1024, 512), 0) == origin[None, :]).astype(BF)
        packed = (mm(keep, pack[:512]) + mm(got, pack[512:])).astype(BF)
        slots = lax.broadcasted_iota(jnp.int32, (512, 1024), 0)
        total = None
        for dz in (0, 1):
            for step in (0, 1, 2, 3):
                piece = rows(packed, (y + step) % 4 * 256 + (zh ^ dz) * 128, 128)
                if dz or step:
                    piece = move(piece, to_chip(step, dz))
                there = chip == (zh ^ dz) * 4 + (y - step) % 4
                select = (slots == jnp.where(there, rank - base, -1)[None, :]).astype(BF)
                term = mm(piece, select)
                total = term if total is None else total + term
        return total

    picked = exchange(0)
    picked = lax.cond(
        jnp.max(rank) >= 512,
        lambda value: value + exchange(512),
        lambda value: value,
        picked,
    )
    cols = (picked * rescale[None, :]).astype(BF)
    cols = jnp.concatenate([mm(cols[:, :512], inverses[0]).astype(BF), cols[:, 512:]], axis=1)

    pair = jnp.concatenate([cols, move(cols, other_zh)], axis=0)

    first = zh * 2 + y // 2
    part = zl ^ (y % 2) ^ zh
    piece = move(cols, to_strip)
    strip = jnp.concatenate([piece, move(piece, other_zl)], axis=0)
    strips = [strip] + [move(strip, along_x(step)) for step in (1, 3)]
    across = move(piece, along_x(2))
    strips += [across, move(across, other_zl)]

    beyond = move(cols, along_y(2))
    near = [pair] + [move(pair, along_y(step)) for step in (1, 3)]
    near += [beyond, move(beyond, other_zh)]
    far = [move(value, other_core) for value in near]

    fp = pair[:, :512]
    right = lax.dynamic_slice_in_dim(pair, 512 + zh * 256, 256, 1)
    gram = lax.dot_general(fp, right, (((0,), (0,)), ((), ())), preferred_element_type=F32)
    gram = rows(gram, k * 256, 256) + move(rows(gram, (1 - k) * 256, 256), other_core)
    odd, high = y % 2, y // 2
    total = rows(gram, odd * 128, 128) + move(rows(gram, (1 - odd) * 128, 128), flip_y(1))
    total = rows(total, high * 64, 64) + move(rows(total, (1 - high) * 64, 64), flip_y(2))
    total = total + move(total, other_zl)
    one, two, three = [move(total, flip_x(bit)) for bit in (1, 2, 3)]
    total = (total + one) + (two + three)
    low = total.astype(BF)
    low = joined(low, move(low, other_zh), zh, 1)
    low = joined(low, move(low, flip_y(2)), high, 0)
    low = joined(low, move(low, flip_y(1)), odd, 0)
    grams = [low, move(low, other_core)]

    index = lax.iota(jnp.int32, 24)
    kind, index = index // 8, index % 8
    hop = jnp.where(index < 6, (index // 2 * (index // 2 + 1)) // 2, 2)
    lower = jnp.where(kind == 0, part, zh) ^ (index % 2)
    base = jnp.where(kind == 0, x - first, y)
    spot = (base - hop) % 4 * 2 + lower
    spot += jnp.where(kind == 0, 0, jnp.where(kind == 1, k, 1 - k)) * 8
    spot = jnp.concatenate([spot, jnp.stack([k, 1 - k]) * 2])
    return tail(spot, strips + near + far + grams, inverses, signed[None, :], trailing)


def solution(mesh):
    placed = (P("row", "col"), P(), P(), P(), P(), P(), P("row", "col"))
    return jax.shard_map(
        body,
        mesh=mesh,
        in_specs=placed,
        out_specs=(P("row", "col"), P("row", None)),
        check_vma=False,
    )
```

```python
import jax
import jax.numpy as jnp
from jax import lax
from jax.experimental import pallas as pl
from jax.experimental.pallas import tpu as pltpu
from jax.sharding import PartitionSpec as P


BF = jnp.bfloat16
F32 = jnp.float32


def move(value, route):
    pairs = []
    for x in range(4):
        for zl in range(2):
            for zh in range(2):
                for y in range(4):
                    for k in range(2):
                        x2, zl2, zh2, y2, k2 = route(x, zl, zh, y, k)
                        source = (x * 2 + zl) * 16 + zh * 8 + y * 2 + k
                        target = (x2 % 4 * 2 + zl2) * 16 + zh2 * 8 + y2 % 4 * 2 + k2
                        pairs.append((source, target))
    return lax.ppermute(value, ("row", "col"), pairs)


def other_core(x, zl, zh, y, k):
    return x, zl, zh, y, 1 - k


def other_zh(x, zl, zh, y, k):
    return x, zl, 1 - zh, y, k


def other_zl(x, zl, zh, y, k):
    return x, 1 - zl, zh, y, k


def along_y(step):
    return lambda x, zl, zh, y, k: (x, zl, zh, y + step, k)


def along_x(step):
    return lambda x, zl, zh, y, k: (x + step, zl, zh, y, k)


def flip_x(bit):
    return lambda x, zl, zh, y, k: (x ^ bit, zl, zh, y, k)


def to_strip(x, zl, zh, y, k):
    zh2 = x // 2
    return x + y, zh ^ zl ^ zh2, zh2, (x % 2) * 2 + zl, k


def rows(value, start, count):
    return lax.dynamic_slice_in_dim(value, start, count, 0)


def put(buffer, piece, start):
    return lax.dynamic_update_slice_in_dim(buffer, piece, start, 0)


def joined(mine, theirs, mine_second, axis):
    return jnp.where(
        mine_second == 1,
        jnp.concatenate([theirs, mine], axis),
        jnp.concatenate([mine, theirs], axis),
    )


def mm(a, b):
    return jnp.dot(a, b, preferred_element_type=F32)


def to_chip(step, dz):
    return lambda x, zl, zh, y, k: (x, zl, zh ^ dz, y + step, k)


def second_panel(cols, inverse, gram, sign):
    weighted = cols[:, :512] * sign[:, :512]
    coupled = (cols[:, 512:].astype(F32) - mm(weighted, gram[...])).astype(BF)
    return mm(coupled, inverse[...]).astype(BF)


SLAB = 512
SLABS = 2048 // SLAB


def tail_kernel(spot, *refs):
    pieces = refs[:17]
    inverses, sign, trailing, out, panels = refs[17:22]
    cols, strip, block, slab, gram_here, inverse_here = refs[22:28]
    piece_sem, fixed_sem, load_sem, save_sem, panel_sem = refs[28:]

    def fetch(i):
        if i >= 24:
            source, target, height = pieces[15 + i - 24], gram_here, 256
        else:
            group, half = i // 8, i % 8
            source = pieces[group * 5 + (half // 2 if half < 6 else half - 3)]
            if half < 6:
                source = source.at[pl.ds(half % 2 * 128, 128)]
            target, height = cols if group == 0 else block, 128
        at = pl.ds(pl.multiple_of(spot[i] * 128, 128), height)
        return pltpu.make_async_copy(source, target.at[at], piece_sem.at[i])

    def rows_of(i):
        return pl.ds(pl.multiple_of(i * SLAB, SLAB), SLAB)

    def load(i):
        return pltpu.make_async_copy(
            trailing.at[rows_of(i)], slab.at[rows_of(i)], load_sem.at[i]
        )

    def save(i):
        return pltpu.make_async_copy(slab.at[rows_of(i)], out.at[rows_of(i)], save_sem.at[i])

    def save_panel(i):
        return pltpu.make_async_copy(
            block.at[rows_of(i)], panels.at[rows_of(i)], panel_sem.at[i]
        )

    constants = pltpu.make_async_copy(inverses.at[1], inverse_here, fixed_sem)
    constants.start()
    early = (*range(8), 24, 25)
    for i in early:
        fetch(i).start()
    for i in range(8, 24):
        fetch(i).start()
    for i in range(SLABS):
        load(i).start()

    for i in early:
        fetch(i).wait()
    constants.wait()
    second = second_panel(cols, inverse_here, gram_here, sign[...])
    strip[:, :512] = cols[:, :512] * sign[:, :512]
    strip[:, 512:] = second * sign[:, 512:]
    for i in range(8, 24):
        fetch(i).wait()

    def step(i, carry):
        at = rows_of(i)
        block[at, 512:] = second_panel(block.at[at], inverse_here, gram_here, sign[...])
        save_panel(i).start()
        load(i).wait()
        slab[at, :] = slab[at, :] + lax.dot_general(
            block[at, :],
            strip[...],
            (((1,), (1,)), ((), ())),
            preferred_element_type=F32,
        )
        save(i).start()
        return carry

    lax.fori_loop(0, SLABS, step, 0)
    for i in range(SLABS):
        save_panel(i).wait()
        save(i).wait()


def tail(spot, pieces, inverses, sign, trailing):
    anywhere = pl.BlockSpec(memory_space=pl.ANY)
    return pl.pallas_call(
        tail_kernel,
        grid_spec=pltpu.PrefetchScalarGridSpec(
            num_scalar_prefetch=1,
            grid=(1,),
            in_specs=[anywhere] * 18
            + [pl.BlockSpec((1, 1024), lambda t, spot: (0, 0)), anywhere],
            out_specs=[anywhere] * 2,
            scratch_shapes=[
                pltpu.VMEM((1024, 1024), BF),
                pltpu.VMEM((1024, 1024), BF),
                pltpu.VMEM((2048, 1024), BF),
                pltpu.VMEM((2048, 1024), F32),
                pltpu.VMEM((512, 512), BF),
                pltpu.VMEM((512, 512), BF),
                pltpu.SemaphoreType.DMA((26,)),
                pltpu.SemaphoreType.DMA,
                pltpu.SemaphoreType.DMA((SLABS,)),
                pltpu.SemaphoreType.DMA((SLABS,)),
                pltpu.SemaphoreType.DMA((SLABS,)),
            ],
        ),
        out_shape=(
            jax.ShapeDtypeStruct((2048, 1024), F32),
            jax.ShapeDtypeStruct((2048, 1024), BF),
        ),
        compiler_params=pltpu.CompilerParams(vmem_limit_bytes=46 * 2**20),
        cost_estimate=pl.CostEstimate(
            flops=9_000_000_000, bytes_accessed=28 * 2**20, transcendentals=0
        ),
    )(spot, *pieces, inverses, sign, trailing)


def body(a_cols, owners, column_slot, update_flag, rescale, inverses, trailing):
    col = lax.axis_index("col")
    row = lax.axis_index("row")
    k, y, zh = col % 2, (col // 2) % 4, col // 8
    x, zl = row // 2, row % 2
    signed = (2 * update_flag - 1).astype(BF)

    keep = rows(a_cols, k * 1024, 1024)
    got = move(rows(a_cols, (1 - k) * 1024, 1024), other_core)
    chip = owners // 2
    stored = (owners % 2 ^ k) * 512 + column_slot
    square = (1024, 1024)
    before = lax.broadcasted_iota(jnp.int32, square, 0) < lax.broadcasted_iota(jnp.int32, square, 1)
    rank = jnp.sum((chip[:, None] == chip[None, :]) & before, axis=0, dtype=jnp.int32)

    def exchange(base):
        slot = lax.broadcasted_iota(jnp.int32, (1024, 512), 1)
        held = (chip == zh * 4 + y)[:, None] & ((rank - base)[:, None] == slot)
        origin = jnp.sum(jnp.where(held, stored[:, None] + 1, 0), axis=0) - 1
        pack = (lax.broadcasted_iota(jnp.int32, (1024, 512), 0) == origin[None, :]).astype(BF)
        packed = (mm(keep, pack[:512]) + mm(got, pack[512:])).astype(BF)
        slots = lax.broadcasted_iota(jnp.int32, (512, 1024), 0)
        total = None
        for dz in (0, 1):
            for step in (0, 1, 2, 3):
                piece = rows(packed, (y + step) % 4 * 256 + (zh ^ dz) * 128, 128)
                if dz or step:
                    piece = move(piece, to_chip(step, dz))
                there = chip == (zh ^ dz) * 4 + (y - step) % 4
                select = (slots == jnp.where(there, rank - base, -1)[None, :]).astype(BF)
                term = mm(piece, select)
                total = term if total is None else total + term
        return total

    picked = exchange(0)
    picked = lax.cond(
        jnp.max(rank) >= 512,
        lambda value: value + exchange(512),
        lambda value: value,
        picked,
    )
    cols = (picked * rescale[None, :]).astype(BF)
    cols = jnp.concatenate([mm(cols[:, :512], inverses[0]).astype(BF), cols[:, 512:]], axis=1)

    pair = jnp.concatenate([cols, move(cols, other_zh)], axis=0)

    first = zh * 2 + y // 2
    part = zl ^ (y % 2) ^ zh
    piece = move(cols, to_strip)
    strip = jnp.concatenate([piece, move(piece, other_zl)], axis=0)
    strips = [strip] + [move(strip, along_x(step)) for step in (1, 3)]
    across = move(piece, along_x(2))
    strips += [across, move(across, other_zl)]

    beyond = move(cols, along_y(2))
    near = [pair] + [move(pair, along_y(step)) for step in (1, 3)]
    near += [beyond, move(beyond, other_zh)]
    far = [move(value, other_core) for value in near]

    fp = pair[:, :512]
    right = lax.dynamic_slice_in_dim(pair, 512 + zh * 256, 256, 1)
    gram = lax.dot_general(fp, right, (((0,), (0,)), ((), ())), preferred_element_type=F32)
    gram = rows(gram, k * 256, 256) + move(rows(gram, (1 - k) * 256, 256), other_core)
    total = rows(gram, y * 64, 64)
    for step in (1, 2, 3):
        total = total + move(rows(gram, ((y + step) % 4) * 64, 64), along_y(step))
    total = total + move(total, other_zl)
    one, two, three = [move(total, flip_x(bit)) for bit in (1, 2, 3)]
    total = (total + one) + (two + three)
    low = total.astype(BF)
    low = joined(low, move(low, other_zh), zh, 1)
    whole = put(jnp.zeros((256, 512), BF), low, y * 64)
    for step in (1, 2, 3):
        whole = put(whole, move(low, along_y(step)), ((y - step) % 4) * 64)
    low = whole
    grams = [low, move(low, other_core)]

    index = lax.iota(jnp.int32, 24)
    kind, index = index // 8, index % 8
    hop = jnp.where(index < 6, (index // 2 * (index // 2 + 1)) // 2, 2)
    lower = jnp.where(kind == 0, part, zh) ^ (index % 2)
    base = jnp.where(kind == 0, x - first, y)
    spot = (base - hop) % 4 * 2 + lower
    spot += jnp.where(kind == 0, 0, jnp.where(kind == 1, k, 1 - k)) * 8
    spot = jnp.concatenate([spot, jnp.stack([k, 1 - k]) * 2])
    return tail(spot, strips + near + far + grams, inverses, signed[None, :], trailing)


def solution(mesh):
    placed = (P("row", "col"), P(), P(), P(), P(), P(), P("row", "col"))
    return jax.shard_map(
        body,
        mesh=mesh,
        in_specs=placed,
        out_specs=(P("row", "col"), P("row", None)),
        check_vma=False,
    )
```

```python
import jax
import jax.numpy as jnp
from jax import lax
from jax.experimental import pallas as pl
from jax.experimental.pallas import tpu as pltpu
from jax.sharding import PartitionSpec as P


BF = jnp.bfloat16
F32 = jnp.float32


def move(value, route):
    pairs = []
    for x in range(4):
        for zl in range(2):
            for zh in range(2):
                for y in range(4):
                    for k in range(2):
                        x2, zl2, zh2, y2, k2 = route(x, zl, zh, y, k)
                        source = (x * 2 + zl) * 16 + zh * 8 + y * 2 + k
                        target = (x2 % 4 * 2 + zl2) * 16 + zh2 * 8 + y2 % 4 * 2 + k2
                        pairs.append((source, target))
    return lax.ppermute(value, ("row", "col"), pairs)


def other_core(x, zl, zh, y, k):
    return x, zl, zh, y, 1 - k


def other_zh(x, zl, zh, y, k):
    return x, zl, 1 - zh, y, k


def other_zl(x, zl, zh, y, k):
    return x, 1 - zl, zh, y, k


def along_y(step):
    return lambda x, zl, zh, y, k: (x, zl, zh, y + step, k)


def along_x(step):
    return lambda x, zl, zh, y, k: (x + step, zl, zh, y, k)


def flip_x(bit):
    return lambda x, zl, zh, y, k: (x ^ bit, zl, zh, y, k)


def to_strip(x, zl, zh, y, k):
    zh2 = x // 2
    return x + y, zh ^ zl ^ zh2, zh2, (x % 2) * 2 + zl, k


def rows(value, start, count):
    return lax.dynamic_slice_in_dim(value, start, count, 0)


def joined(mine, theirs, mine_second, axis):
    return jnp.where(
        mine_second == 1,
        jnp.concatenate([theirs, mine], axis),
        jnp.concatenate([mine, theirs], axis),
    )


def mm(a, b):
    return jnp.dot(a, b, preferred_element_type=F32)


def to_chip(step, dz):
    return lambda x, zl, zh, y, k: (x, zl, zh ^ dz, y + step, k)


def second_panel(cols, inverse, gram, sign):
    weighted = cols[:, :512] * sign[:, :512]
    coupled = (cols[:, 512:].astype(F32) - mm(weighted, gram[...])).astype(BF)
    return mm(coupled, inverse[...]).astype(BF)


SLAB = 512
SLABS = 2048 // SLAB


def tail_kernel(spot, *refs):
    pieces = refs[:17]
    inverses, sign, trailing, out, panels = refs[17:22]
    cols, strip, block, slab, gram_here, inverse_here = refs[22:28]
    piece_sem, fixed_sem, load_sem, save_sem, panel_sem = refs[28:]

    def fetch(i):
        if i >= 24:
            source = pieces[15 + (i - 24) // 4].at[pl.ds(i % 4 * 64, 64)]
            target, height = gram_here, 64
        else:
            group, half = i // 8, i % 8
            source = pieces[group * 5 + (half // 2 if half < 6 else half - 3)]
            if half < 6:
                source = source.at[pl.ds(half % 2 * 128, 128)]
            target, height = cols if group == 0 else block, 128
        at = pl.ds(pl.multiple_of(spot[i] * 64, height), height)
        return pltpu.make_async_copy(source, target.at[at], piece_sem.at[i])

    def rows_of(i):
        return pl.ds(pl.multiple_of(i * SLAB, SLAB), SLAB)

    def load(i):
        return pltpu.make_async_copy(
            trailing.at[rows_of(i)], slab.at[rows_of(i)], load_sem.at[i]
        )

    def save(i):
        return pltpu.make_async_copy(slab.at[rows_of(i)], out.at[rows_of(i)], save_sem.at[i])

    def save_panel(i):
        return pltpu.make_async_copy(
            block.at[rows_of(i)], panels.at[rows_of(i)], panel_sem.at[i]
        )

    constants = pltpu.make_async_copy(inverses.at[1], inverse_here, fixed_sem)
    constants.start()
    early = (*range(8), *range(24, 32))
    for i in early:
        fetch(i).start()
    for i in range(8, 24):
        fetch(i).start()
    for i in range(SLABS):
        load(i).start()

    for i in early:
        fetch(i).wait()
    constants.wait()
    second = second_panel(cols, inverse_here, gram_here, sign[...])
    strip[:, :512] = cols[:, :512] * sign[:, :512]
    strip[:, 512:] = second * sign[:, 512:]
    for i in range(8, 24):
        fetch(i).wait()

    def step(i, carry):
        at = rows_of(i)
        block[at, 512:] = second_panel(block.at[at], inverse_here, gram_here, sign[...])
        save_panel(i).start()
        load(i).wait()
        slab[at, :] = slab[at, :] + lax.dot_general(
            block[at, :],
            strip[...],
            (((1,), (1,)), ((), ())),
            preferred_element_type=F32,
        )
        save(i).start()
        return carry

    lax.fori_loop(0, SLABS, step, 0)
    for i in range(SLABS):
        save_panel(i).wait()
        save(i).wait()


def tail(spot, pieces, inverses, sign, trailing):
    anywhere = pl.BlockSpec(memory_space=pl.ANY)
    return pl.pallas_call(
        tail_kernel,
        grid_spec=pltpu.PrefetchScalarGridSpec(
            num_scalar_prefetch=1,
            grid=(1,),
            in_specs=[anywhere] * 18
            + [pl.BlockSpec((1, 1024), lambda t, spot: (0, 0)), anywhere],
            out_specs=[anywhere] * 2,
            scratch_shapes=[
                pltpu.VMEM((1024, 1024), BF),
                pltpu.VMEM((1024, 1024), BF),
                pltpu.VMEM((2048, 1024), BF),
                pltpu.VMEM((2048, 1024), F32),
                pltpu.VMEM((512, 512), BF),
                pltpu.VMEM((512, 512), BF),
                pltpu.SemaphoreType.DMA((32,)),
                pltpu.SemaphoreType.DMA,
                pltpu.SemaphoreType.DMA((SLABS,)),
                pltpu.SemaphoreType.DMA((SLABS,)),
                pltpu.SemaphoreType.DMA((SLABS,)),
            ],
        ),
        out_shape=(
            jax.ShapeDtypeStruct((2048, 1024), F32),
            jax.ShapeDtypeStruct((2048, 1024), BF),
        ),
        compiler_params=pltpu.CompilerParams(vmem_limit_bytes=46 * 2**20),
        cost_estimate=pl.CostEstimate(
            flops=9_000_000_000, bytes_accessed=28 * 2**20, transcendentals=0
        ),
    )(spot, *pieces, inverses, sign, trailing)


def body(a_cols, owners, column_slot, update_flag, rescale, inverses, trailing):
    col = lax.axis_index("col")
    row = lax.axis_index("row")
    k, y, zh = col % 2, (col // 2) % 4, col // 8
    x, zl = row // 2, row % 2
    signed = (2 * update_flag - 1).astype(BF)

    keep = rows(a_cols, k * 1024, 1024)
    got = move(rows(a_cols, (1 - k) * 1024, 1024), other_core)
    chip = owners // 2
    stored = (owners % 2 ^ k) * 512 + column_slot
    square = (1024, 1024)
    before = lax.broadcasted_iota(jnp.int32, square, 0) < lax.broadcasted_iota(jnp.int32, square, 1)
    rank = jnp.sum((chip[:, None] == chip[None, :]) & before, axis=0, dtype=jnp.int32)

    def exchange(base):
        slot = lax.broadcasted_iota(jnp.int32, (1024, 512), 1)
        held = (chip == zh * 4 + y)[:, None] & ((rank - base)[:, None] == slot)
        origin = jnp.sum(jnp.where(held, stored[:, None] + 1, 0), axis=0) - 1
        pack = (lax.broadcasted_iota(jnp.int32, (1024, 512), 0) == origin[None, :]).astype(BF)
        packed = (mm(keep, pack[:512]) + mm(got, pack[512:])).astype(BF)
        slots = lax.broadcasted_iota(jnp.int32, (512, 1024), 0)
        total = None
        for dz in (0, 1):
            for step in (0, 1, 2, 3):
                piece = rows(packed, (y + step) % 4 * 256 + (zh ^ dz) * 128, 128)
                if dz or step:
                    piece = move(piece, to_chip(step, dz))
                there = chip == (zh ^ dz) * 4 + (y - step) % 4
                select = (slots == jnp.where(there, rank - base, -1)[None, :]).astype(BF)
                term = mm(piece, select)
                total = term if total is None else total + term
        return total

    picked = exchange(0)
    picked = lax.cond(
        jnp.max(rank) >= 512,
        lambda value: value + exchange(512),
        lambda value: value,
        picked,
    )
    cols = (picked * rescale[None, :]).astype(BF)
    cols = jnp.concatenate([mm(cols[:, :512], inverses[0]).astype(BF), cols[:, 512:]], axis=1)

    pair = jnp.concatenate([cols, move(cols, other_zh)], axis=0)

    first = zh * 2 + y // 2
    part = zl ^ (y % 2) ^ zh
    piece = move(cols, to_strip)
    strip = jnp.concatenate([piece, move(piece, other_zl)], axis=0)
    strips = [strip] + [move(strip, along_x(step)) for step in (1, 3)]
    across = move(piece, along_x(2))
    strips += [across, move(across, other_zl)]

    beyond = move(cols, along_y(2))
    near = [pair] + [move(pair, along_y(step)) for step in (1, 3)]
    near += [beyond, move(beyond, other_zh)]
    far = [move(value, other_core) for value in near]

    fp = pair[:, :512]
    right = lax.dynamic_slice_in_dim(pair, 512 + zh * 256, 256, 1)
    gram = lax.dot_general(fp, right, (((0,), (0,)), ((), ())), preferred_element_type=F32)
    gram = rows(gram, k * 256, 256) + move(rows(gram, (1 - k) * 256, 256), other_core)
    total = rows(gram, y * 64, 64)
    for step in (1, 2, 3):
        total = total + move(rows(gram, ((y + step) % 4) * 64, 64), along_y(step))
    total = total + move(total, other_zl)
    one, two, three = [move(total, flip_x(bit)) for bit in (1, 2, 3)]
    total = (total + one) + (two + three)
    low = total.astype(BF)
    low = joined(low, move(low, other_zh), zh, 1)
    ring = [low] + [move(low, along_y(step)) for step in (1, 2, 3)]
    low = jnp.concatenate(ring, axis=0)
    grams = [low, move(low, other_core)]

    index = lax.iota(jnp.int32, 24)
    kind, index = index // 8, index % 8
    hop = jnp.where(index < 6, (index // 2 * (index // 2 + 1)) // 2, 2)
    lower = jnp.where(kind == 0, part, zh) ^ (index % 2)
    base = jnp.where(kind == 0, x - first, y)
    spot = (base - hop) % 4 * 2 + lower
    spot += jnp.where(kind == 0, 0, jnp.where(kind == 1, k, 1 - k)) * 8
    chunk = lax.iota(jnp.int32, 8)
    chunk = jnp.where(chunk < 4, k, 1 - k) * 4 + (y - chunk) % 4
    spot = jnp.concatenate([spot * 2, chunk])
    return tail(spot, strips + near + far + grams, inverses, signed[None, :], trailing)


def solution(mesh):
    placed = (P("row", "col"), P(), P(), P(), P(), P(), P("row", "col"))
    return jax.shard_map(
        body,
        mesh=mesh,
        in_specs=placed,
        out_specs=(P("row", "col"), P("row", None)),
        check_vma=False,
    )
```

```python
import jax
import jax.numpy as jnp
from jax import lax
from jax.experimental import pallas as pl
from jax.experimental.pallas import tpu as pltpu
from jax.sharding import PartitionSpec as P


BF = jnp.bfloat16
F32 = jnp.float32


def move(value, route):
    pairs = []
    for x in range(4):
        for zl in range(2):
            for zh in range(2):
                for y in range(4):
                    for k in range(2):
                        x2, zl2, zh2, y2, k2 = route(x, zl, zh, y, k)
                        source = (x * 2 + zl) * 16 + zh * 8 + y * 2 + k
                        target = (x2 % 4 * 2 + zl2) * 16 + zh2 * 8 + y2 % 4 * 2 + k2
                        pairs.append((source, target))
    return lax.ppermute(value, ("row", "col"), pairs)


def other_core(x, zl, zh, y, k):
    return x, zl, zh, y, 1 - k


def other_zh(x, zl, zh, y, k):
    return x, zl, 1 - zh, y, k


def other_zl(x, zl, zh, y, k):
    return x, 1 - zl, zh, y, k


def along_y(step):
    return lambda x, zl, zh, y, k: (x, zl, zh, y + step, k)


def along_x(step):
    return lambda x, zl, zh, y, k: (x + step, zl, zh, y, k)


def flip_x(bit):
    return lambda x, zl, zh, y, k: (x ^ bit, zl, zh, y, k)


def to_strip(x, zl, zh, y, k):
    zh2 = x // 2
    return x + y, zh ^ zl ^ zh2, zh2, (x % 2) * 2 + zl, k


def rows(value, start, count):
    return lax.dynamic_slice_in_dim(value, start, count, 0)


def joined(mine, theirs, mine_second, axis):
    return jnp.where(
        mine_second == 1,
        jnp.concatenate([theirs, mine], axis),
        jnp.concatenate([mine, theirs], axis),
    )


def put(buffer, piece, start):
    return lax.dynamic_update_slice_in_dim(buffer, piece, start, 0)


def mm(a, b):
    return jnp.dot(a, b, preferred_element_type=F32)


def to_chip(step, dz):
    return lambda x, zl, zh, y, k: (x, zl, zh ^ dz, y + step, k)


def second_panel(cols, inverse, gram, sign):
    weighted = cols[:, :512] * sign[:, :512]
    coupled = (cols[:, 512:].astype(F32) - mm(weighted, gram[...])).astype(BF)
    return mm(coupled, inverse[...]).astype(BF)


SLAB = 512
SLABS = 2048 // SLAB


def tail_kernel(spot, *refs):
    pieces = refs[:17]
    inverses, sign, trailing, out, panels = refs[17:22]
    cols, strip, block, slab, gram_here, inverse_here = refs[22:28]
    piece_sem, fixed_sem, load_sem, save_sem, panel_sem = refs[28:]

    def fetch(i):
        height = pieces[i].shape[0]
        at = pl.ds(pl.multiple_of(spot[i] * 128, 128), height)
        target = cols if i < 5 else block if i < 15 else gram_here
        return pltpu.make_async_copy(pieces[i], target.at[at], piece_sem.at[i])

    def rows_of(i):
        return pl.ds(pl.multiple_of(i * SLAB, SLAB), SLAB)

    def load(i):
        return pltpu.make_async_copy(
            trailing.at[rows_of(i)], slab.at[rows_of(i)], load_sem.at[i]
        )

    def save(i):
        return pltpu.make_async_copy(slab.at[rows_of(i)], out.at[rows_of(i)], save_sem.at[i])

    def save_panel(i):
        return pltpu.make_async_copy(
            block.at[rows_of(i)], panels.at[rows_of(i)], panel_sem.at[i]
        )

    constants = pltpu.make_async_copy(inverses.at[1], inverse_here, fixed_sem)
    constants.start()
    early = (0, 1, 2, 3, 4, 15, 16)
    for i in early:
        fetch(i).start()
    for i in range(5, 15):
        fetch(i).start()
    for i in range(SLABS):
        load(i).start()

    for i in early:
        fetch(i).wait()
    constants.wait()
    second = second_panel(cols, inverse_here, gram_here, sign[...])
    strip[:, :512] = cols[:, :512] * sign[:, :512]
    strip[:, 512:] = second * sign[:, 512:]
    for i in range(5, 15):
        fetch(i).wait()

    def step(i, carry):
        at = rows_of(i)
        block[at, 512:] = second_panel(block.at[at], inverse_here, gram_here, sign[...])
        save_panel(i).start()
        load(i).wait()
        slab[at, :] = slab[at, :] + lax.dot_general(
            block[at, :],
            strip[...],
            (((1,), (1,)), ((), ())),
            preferred_element_type=F32,
        )
        save(i).start()
        return carry

    lax.fori_loop(0, SLABS, step, 0)
    for i in range(SLABS):
        save_panel(i).wait()
        save(i).wait()


def tail(spot, pieces, inverses, sign, trailing):
    anywhere = pl.BlockSpec(memory_space=pl.ANY)
    return pl.pallas_call(
        tail_kernel,
        grid_spec=pltpu.PrefetchScalarGridSpec(
            num_scalar_prefetch=1,
            grid=(1,),
            in_specs=[anywhere] * 18
            + [pl.BlockSpec((1, 1024), lambda t, spot: (0, 0)), anywhere],
            out_specs=[anywhere] * 2,
            scratch_shapes=[
                pltpu.VMEM((1024, 1024), BF),
                pltpu.VMEM((1024, 1024), BF),
                pltpu.VMEM((2048, 1024), BF),
                pltpu.VMEM((2048, 1024), F32),
                pltpu.VMEM((512, 512), BF),
                pltpu.VMEM((512, 512), BF),
                pltpu.SemaphoreType.DMA((17,)),
                pltpu.SemaphoreType.DMA,
                pltpu.SemaphoreType.DMA((SLABS,)),
                pltpu.SemaphoreType.DMA((SLABS,)),
                pltpu.SemaphoreType.DMA((SLABS,)),
            ],
        ),
        out_shape=(
            jax.ShapeDtypeStruct((2048, 1024), F32),
            jax.ShapeDtypeStruct((2048, 1024), BF),
        ),
        compiler_params=pltpu.CompilerParams(vmem_limit_bytes=46 * 2**20),
        cost_estimate=pl.CostEstimate(
            flops=9_000_000_000, bytes_accessed=28 * 2**20, transcendentals=0
        ),
    )(spot, *pieces, inverses, sign, trailing)


def body(a_cols, owners, column_slot, update_flag, rescale, inverses, trailing):
    col = lax.axis_index("col")
    row = lax.axis_index("row")
    k, y, zh = col % 2, (col // 2) % 4, col // 8
    x, zl = row // 2, row % 2
    signed = (2 * update_flag - 1).astype(BF)

    keep = rows(a_cols, k * 1024, 1024)
    got = move(rows(a_cols, (1 - k) * 1024, 1024), other_core)
    chip = owners // 2
    stored = (owners % 2 ^ k) * 512 + column_slot
    square = (1024, 1024)
    before = lax.broadcasted_iota(jnp.int32, square, 0) < lax.broadcasted_iota(jnp.int32, square, 1)
    rank = jnp.sum((chip[:, None] == chip[None, :]) & before, axis=0, dtype=jnp.int32)

    def exchange(base):
        slot = lax.broadcasted_iota(jnp.int32, (1024, 512), 1)
        held = (chip == zh * 4 + y)[:, None] & ((rank - base)[:, None] == slot)
        origin = jnp.sum(jnp.where(held, stored[:, None] + 1, 0), axis=0) - 1
        pack = (lax.broadcasted_iota(jnp.int32, (1024, 512), 0) == origin[None, :]).astype(BF)
        packed = (mm(keep, pack[:512]) + mm(got, pack[512:])).astype(BF)
        slots = lax.broadcasted_iota(jnp.int32, (512, 1024), 0)
        total = None
        for dz in (0, 1):
            for step in (0, 1, 2, 3):
                piece = rows(packed, (y + step) % 4 * 256 + (zh ^ dz) * 128, 128)
                if dz or step:
                    piece = move(piece, to_chip(step, dz))
                there = chip == (zh ^ dz) * 4 + (y - step) % 4
                select = (slots == jnp.where(there, rank - base, -1)[None, :]).astype(BF)
                term = mm(piece, select)
                total = term if total is None else total + term
        return total

    picked = exchange(0)
    picked = lax.cond(
        jnp.max(rank) >= 512,
        lambda value: value + exchange(512),
        lambda value: value,
        picked,
    )
    cols = (picked * rescale[None, :]).astype(BF)
    cols = cols.at[:, :512].set(mm(cols[:, :512], inverses[0]).astype(BF))

    pair = put(jnp.zeros((256, 1024), BF), cols, zh * 128)
    pair = put(pair, move(cols, other_zh), (1 - zh) * 128)

    first = zh * 2 + y // 2
    part = zl ^ (y % 2) ^ zh
    piece = move(cols, to_strip)
    strip = put(jnp.zeros((256, 1024), BF), piece, part * 128)
    strip = put(strip, move(piece, other_zl), (1 - part) * 128)
    strips = [strip] + [move(strip, along_x(step)) for step in (1, 3)]
    across = move(piece, along_x(2))
    strips += [across, move(across, other_zl)]

    beyond = move(cols, along_y(2))
    near = [pair] + [move(pair, along_y(step)) for step in (1, 3)]
    near += [beyond, move(beyond, other_zh)]
    far = [move(value, other_core) for value in near]

    fp = pair[:, :512]
    right = lax.dynamic_slice_in_dim(pair, 512 + zh * 256, 256, 1)
    gram = lax.dot_general(fp, right, (((0,), (0,)), ((), ())), preferred_element_type=F32)
    gram = rows(gram, k * 256, 256) + move(rows(gram, (1 - k) * 256, 256), other_core)
    total = rows(gram, y * 64, 64)
    for step in (1, 2, 3):
        total = total + move(rows(gram, ((y + step) % 4) * 64, 64), along_y(step))
    total = total + move(total, other_zl)
    one, two, three = [move(total, flip_x(bit)) for bit in (1, 2, 3)]
    total = (total + one) + (two + three)
    low = total.astype(BF)
    low2 = joined(low, move(low, other_zh), zh, 1)
    low3 = put(jnp.zeros((256, 512), BF), low2, y * 64)
    for step in (1, 2, 3):
        low3 = put(low3, move(low2, along_y(step)), ((y - step) % 4) * 64)
    grams = [low3, move(low3, other_core)]

    index = lax.iota(jnp.int32, 15)
    kind, index = index // 5, index % 5
    hop = jnp.where(index < 3, (index * index + index) // 2, 2)
    half = jnp.where(kind == 0, part, zh)
    lower = jnp.where(index == 3, half, jnp.where(index == 4, 1 - half, 0))
    base = jnp.where(kind == 0, x - first, y)
    spot = (base - hop) % 4 * 2 + lower
    spot += jnp.where(kind == 0, 0, jnp.where(kind == 1, k, 1 - k)) * 8
    spot = jnp.concatenate([spot, jnp.stack([k, 1 - k]) * 2])
    return tail(spot, strips + near + far + grams, inverses, signed[None, :], trailing)


def solution(mesh):
    placed = (P("row", "col"), P(), P(), P(), P(), P(), P("row", "col"))
    return jax.shard_map(
        body,
        mesh=mesh,
        in_specs=placed,
        out_specs=(P("row", "col"), P("row", None)),
        check_vma=False,
    )
```

```python
import jax
import jax.numpy as jnp
from jax import lax
from jax.experimental import pallas as pl
from jax.experimental.pallas import tpu as pltpu
from jax.sharding import PartitionSpec as P


BF = jnp.bfloat16
F32 = jnp.float32


def move(value, route):
    pairs = []
    for x in range(4):
        for zl in range(2):
            for zh in range(2):
                for y in range(4):
                    for k in range(2):
                        x2, zl2, zh2, y2, k2 = route(x, zl, zh, y, k)
                        source = (x * 2 + zl) * 16 + zh * 8 + y * 2 + k
                        target = (x2 % 4 * 2 + zl2) * 16 + zh2 * 8 + y2 % 4 * 2 + k2
                        pairs.append((source, target))
    return lax.ppermute(value, ("row", "col"), pairs)


def other_core(x, zl, zh, y, k):
    return x, zl, zh, y, 1 - k


def other_zh(x, zl, zh, y, k):
    return x, zl, 1 - zh, y, k


def other_zl(x, zl, zh, y, k):
    return x, 1 - zl, zh, y, k


def along_y(step):
    return lambda x, zl, zh, y, k: (x, zl, zh, y + step, k)


def along_x(step):
    return lambda x, zl, zh, y, k: (x + step, zl, zh, y, k)


def flip_x(bit):
    return lambda x, zl, zh, y, k: (x ^ bit, zl, zh, y, k)


def to_strip(x, zl, zh, y, k):
    zh2 = x // 2
    return x + y, zh ^ zl ^ zh2, zh2, (x % 2) * 2 + zl, k


def rows(value, start, count):
    return lax.dynamic_slice_in_dim(value, start, count, 0)


def put(buffer, piece, start):
    return lax.dynamic_update_slice_in_dim(buffer, piece, start, 0)


def mm(a, b):
    return jnp.dot(a, b, preferred_element_type=F32)


def to_chip(step, dz):
    return lambda x, zl, zh, y, k: (x, zl, zh ^ dz, y + step, k)


def second_panel(cols, inverse, gram, sign):
    weighted = cols[:, :512] * sign[:, :512]
    coupled = (cols[:, 512:].astype(F32) - mm(weighted, gram[...])).astype(BF)
    return mm(coupled, inverse[...]).astype(BF)


SLAB = 512
SLABS = 2048 // SLAB


def tail_kernel(spot, *refs):
    pieces = refs[:17]
    inverses, sign, trailing, out, panels = refs[17:22]
    cols, strip, block, slab, gram_here, inverse_here = refs[22:28]
    piece_sem, fixed_sem, load_sem, save_sem, panel_sem = refs[28:]

    def fetch(i):
        height = pieces[i].shape[0]
        at = pl.ds(pl.multiple_of(spot[i] * 128, 128), height)
        target = cols if i < 5 else block if i < 15 else gram_here
        return pltpu.make_async_copy(pieces[i], target.at[at], piece_sem.at[i])

    def rows_of(i):
        return pl.ds(pl.multiple_of(i * SLAB, SLAB), SLAB)

    def load(i):
        return pltpu.make_async_copy(
            trailing.at[rows_of(i)], slab.at[rows_of(i)], load_sem.at[i]
        )

    def save(i):
        return pltpu.make_async_copy(slab.at[rows_of(i)], out.at[rows_of(i)], save_sem.at[i])

    def save_panel(i):
        return pltpu.make_async_copy(
            block.at[rows_of(i)], panels.at[rows_of(i)], panel_sem.at[i]
        )

    constants = pltpu.make_async_copy(inverses.at[1], inverse_here, fixed_sem)
    constants.start()
    early = (0, 1, 2, 3, 4, 15, 16)
    for i in early:
        fetch(i).start()
    for i in range(5, 15):
        fetch(i).start()
    for i in range(SLABS):
        load(i).start()

    for i in early:
        fetch(i).wait()
    constants.wait()
    second = second_panel(cols, inverse_here, gram_here, sign[...])
    strip[:, :512] = cols[:, :512] * sign[:, :512]
    strip[:, 512:] = second * sign[:, 512:]
    for i in range(5, 15):
        fetch(i).wait()

    def step(i, carry):
        at = rows_of(i)
        block[at, 512:] = second_panel(block.at[at], inverse_here, gram_here, sign[...])
        save_panel(i).start()
        load(i).wait()
        slab[at, :] = slab[at, :] + lax.dot_general(
            block[at, :],
            strip[...],
            (((1,), (1,)), ((), ())),
            preferred_element_type=F32,
        )
        save(i).start()
        return carry

    lax.fori_loop(0, SLABS, step, 0)
    for i in range(SLABS):
        save_panel(i).wait()
        save(i).wait()


def tail(spot, pieces, inverses, sign, trailing):
    anywhere = pl.BlockSpec(memory_space=pl.ANY)
    return pl.pallas_call(
        tail_kernel,
        grid_spec=pltpu.PrefetchScalarGridSpec(
            num_scalar_prefetch=1,
            grid=(1,),
            in_specs=[anywhere] * 18
            + [pl.BlockSpec((1, 1024), lambda t, spot: (0, 0)), anywhere],
            out_specs=[anywhere] * 2,
            scratch_shapes=[
                pltpu.VMEM((1024, 1024), BF),
                pltpu.VMEM((1024, 1024), BF),
                pltpu.VMEM((2048, 1024), BF),
                pltpu.VMEM((2048, 1024), F32),
                pltpu.VMEM((512, 512), BF),
                pltpu.VMEM((512, 512), BF),
                pltpu.SemaphoreType.DMA((17,)),
                pltpu.SemaphoreType.DMA,
                pltpu.SemaphoreType.DMA((SLABS,)),
                pltpu.SemaphoreType.DMA((SLABS,)),
                pltpu.SemaphoreType.DMA((SLABS,)),
            ],
        ),
        out_shape=(
            jax.ShapeDtypeStruct((2048, 1024), F32),
            jax.ShapeDtypeStruct((2048, 1024), BF),
        ),
        compiler_params=pltpu.CompilerParams(vmem_limit_bytes=46 * 2**20),
        cost_estimate=pl.CostEstimate(
            flops=9_000_000_000, bytes_accessed=28 * 2**20, transcendentals=0
        ),
    )(spot, *pieces, inverses, sign, trailing)


def body(a_cols, owners, column_slot, update_flag, rescale, inverses, trailing):
    col = lax.axis_index("col")
    row = lax.axis_index("row")
    k, y, zh = col % 2, (col // 2) % 4, col // 8
    x, zl = row // 2, row % 2
    signed = (2 * update_flag - 1).astype(BF)

    keep = rows(a_cols, k * 1024, 1024)
    got = move(rows(a_cols, (1 - k) * 1024, 1024), other_core)
    chip = owners // 2
    stored = (owners % 2 ^ k) * 512 + column_slot
    square = (1024, 1024)
    before = lax.broadcasted_iota(jnp.int32, square, 0) < lax.broadcasted_iota(jnp.int32, square, 1)
    rank = jnp.sum((chip[:, None] == chip[None, :]) & before, axis=0, dtype=jnp.int32)

    def exchange(base):
        slot = lax.broadcasted_iota(jnp.int32, (1024, 512), 1)
        held = (chip == zh * 4 + y)[:, None] & ((rank - base)[:, None] == slot)
        origin = jnp.sum(jnp.where(held, stored[:, None] + 1, 0), axis=0) - 1
        pack = (lax.broadcasted_iota(jnp.int32, (1024, 512), 0) == origin[None, :]).astype(BF)
        packed = (mm(keep, pack[:512]) + mm(got, pack[512:])).astype(BF)
        slots = lax.broadcasted_iota(jnp.int32, (512, 1024), 0)
        total = None
        for dz in (0, 1):
            for step in (0, 1, 2, 3):
                piece = rows(packed, (y + step) % 4 * 256 + (zh ^ dz) * 128, 128)
                if dz or step:
                    piece = move(piece, to_chip(step, dz))
                there = chip == (zh ^ dz) * 4 + (y - step) % 4
                select = (slots == jnp.where(there, rank - base, -1)[None, :]).astype(BF)
                term = mm(piece, select)
                total = term if total is None else total + term
        return total

    picked = exchange(0)
    picked = lax.cond(
        jnp.max(rank) >= 512,
        lambda value: value + exchange(512),
        lambda value: value,
        picked,
    )
    cols = (picked * rescale[None, :]).astype(BF)
    cols = cols.at[:, :512].set(mm(cols[:, :512], inverses[0]).astype(BF))

    pair = put(jnp.zeros((256, 1024), BF), cols, zh * 128)
    pair = put(pair, move(cols, other_zh), (1 - zh) * 128)

    first = zh * 2 + y // 2
    part = zl ^ (y % 2) ^ zh
    piece = move(cols, to_strip)
    strip = put(jnp.zeros((256, 1024), BF), piece, part * 128)
    strip = put(strip, move(piece, other_zl), (1 - part) * 128)
    strips = [strip] + [move(strip, along_x(step)) for step in (1, 3)]
    across = move(piece, along_x(2))
    strips += [across, move(across, other_zl)]

    beyond = move(cols, along_y(2))
    near = [pair] + [move(pair, along_y(step)) for step in (1, 3)]
    near += [beyond, move(beyond, other_zh)]
    far = [move(value, other_core) for value in near]

    fp = pair[:, :512]
    right = lax.dynamic_slice_in_dim(pair, 512 + zh * 256, 256, 1)
    gram = lax.dot_general(fp, right, (((0,), (0,)), ((), ())), preferred_element_type=F32)
    gram = rows(gram, k * 256, 256) + move(rows(gram, (1 - k) * 256, 256), other_core)
    total = rows(gram, y * 64, 64)
    for step in (1, 2, 3):
        total = total + move(rows(gram, ((y + step) % 4) * 64, 64), along_y(step))
    total = total + move(total, other_zl)
    one, two, three = [move(total, flip_x(bit)) for bit in (1, 2, 3)]
    total = (total + one) + (two + three)
    low = total.astype(BF)
    low2 = jnp.zeros((64, 512), BF)
    low2 = lax.dynamic_update_slice_in_dim(low2, low, zh * 256, 1)
    low2 = lax.dynamic_update_slice_in_dim(low2, move(low, other_zh), (1 - zh) * 256, 1)
    low3 = put(jnp.zeros((256, 512), BF), low2, y * 64)
    for step in (1, 2, 3):
        low3 = put(low3, move(low2, along_y(step)), ((y - step) % 4) * 64)
    grams = [low3, move(low3, other_core)]

    index = lax.iota(jnp.int32, 15)
    kind, index = index // 5, index % 5
    hop = jnp.where(index < 3, (index * index + index) // 2, 2)
    half = jnp.where(kind == 0, part, zh)
    lower = jnp.where(index == 3, half, jnp.where(index == 4, 1 - half, 0))
    base = jnp.where(kind == 0, x - first, y)
    spot = (base - hop) % 4 * 2 + lower
    spot += jnp.where(kind == 0, 0, jnp.where(kind == 1, k, 1 - k)) * 8
    spot = jnp.concatenate([spot, jnp.stack([k, 1 - k]) * 2])
    return tail(spot, strips + near + far + grams, inverses, signed[None, :], trailing)


def solution(mesh):
    placed = (P("row", "col"), P(), P(), P(), P(), P(), P("row", "col"))
    return jax.shard_map(
        body,
        mesh=mesh,
        in_specs=placed,
        out_specs=(P("row", "col"), P("row", None)),
        check_vma=False,
    )
```
